512 devices in a mesh: grp: 16 (over y, x_hi), pos: 32 (over x_lo, z, core).
Axes of the slice: x: 4 (x_hi: 2, x_lo: 2; x = x_hi * 2 + x_lo), y: 8, z: 8, core: 2. Of those that a mesh axis runs over, the one named last changes fastest.
Arguments:
- features: bfloat16 [2, 2048, 512, 448], P(None, ('grp', 'pos'))
- channel_index: int32 [100], replicated, may hold values from 0 to 447, as said below
Outputs:
- factor: float32 [512, 100, 100], P('pos')
- mean_vec: float32 [512, 100], P('pos')
The draws below stay inside these ranges and needn't reach their ends.
Inputs may be any that keep to these rules, and one draw needn't show every extreme that they name: `channel_index`: 100 distinct channel numbers; 0 and 447 are always among them.
All inputs are finite; a program needn't handle non-finite values.
Results may differ from the reference program's by a relative error of at most 0.0003.
Values may be sent and summed in bfloat16 or wider, within the bound.
A program may use at most 64 MiB of HBM per device.

```python
import math
import jax
import jax.numpy as jnp
from jax import lax

CH_ALL = 448
KEEP = 100
BATCHES = 2
IMAGES = 2048
POS = 512


def draw_features(key, part):
    keys = jax.random.split(key, 5)
    shape = (BATCHES, IMAGES, POS, CH_ALL)
    noise = jax.random.normal(keys[0], shape, jnp.float32)
    rise = 0.5
    spread = 1.2
    latent = jax.random.normal(keys[1], (BATCHES, IMAGES, POS, CH_ALL // 16), jnp.float32)
    shared = jnp.repeat(latent, 16, axis=3)
    center = jax.random.uniform(keys[2], (POS, CH_ALL), jnp.float32, 0.0, 2.0)
    scale = jnp.exp(jax.random.uniform(keys[3], (POS, CH_ALL), jnp.float32, -spread, spread))
    mixing = jax.random.uniform(keys[4], (POS, CH_ALL), jnp.float32, 0.3, 1.2)
    ramp = jnp.arange(IMAGES, dtype=jnp.float32) / max(IMAGES - 1, 1)
    amplitude = jnp.power(3.0, rise * ramp)[None, :, None, None]
    values = center + amplitude * (scale * noise + mixing * shared)
    return values.astype(jnp.bfloat16)


def draw_channel_index(key, part):
    keys = jax.random.split(key, 2)
    middle = jax.random.permutation(keys[0], CH_ALL - 2)[:KEEP - 2] + 1
    listed = jnp.concatenate([jnp.array([0, CH_ALL - 1], dtype=jnp.int32), middle.astype(jnp.int32)])
    order = jax.random.permutation(keys[1], KEEP)
    return listed[order].astype(jnp.int32)


def setup_inputs(seed: int = 0) -> dict:
    seeds = jax.random.split(jax.random.key(seed), 3)
    features = draw_features(jax.random.fold_in(seeds[2], 71), 0)
    channel_index = draw_channel_index(jax.random.fold_in(seeds[2], 71), 0)
    return dict(features=features, channel_index=channel_index)


RIDGE = 0.01

def reference(features, channel_index):
    block_size = math.gcd(POS, 16)
    starts = jnp.arange(POS // block_size, dtype=jnp.int32) * block_size

    def block_moments(start):
        window = lax.dynamic_slice_in_dim(features, start, block_size, 2)
        chosen = jnp.take(window, channel_index, axis=3).astype(jnp.float32)
        second_moment = jnp.einsum('bipc,bipd->pcd', chosen, chosen, precision=lax.Precision.HIGHEST)
        column_sums = jnp.sum(chosen, axis=(0, 1))
        return (second_moment, column_sums)
    second_moment, column_sums = lax.map(block_moments, starts)
    second_moment = second_moment.reshape(POS, KEEP, KEEP)
    column_sums = column_sums.reshape(POS, KEEP)
    image_total = BATCHES * IMAGES
    mean_vec = column_sums / image_total
    outer = image_total * mean_vec[:, :, None] * mean_vec[:, None, :]
    identity = jnp.eye(KEEP, dtype=jnp.float32)
    covariance = (second_moment - outer) / (image_total - 1) + RIDGE * identity
    factor = jnp.linalg.cholesky(covariance)
    return (factor, mean_vec)
```

```python
import jax
import jax.numpy as jnp
from jax import lax
from jax.experimental import pallas as pl
from jax.experimental.pallas import tpu as pltpu
from jax.sharding import PartitionSpec as P

RIDGE = 0.01
LANES = 128
NX, NY, NZ = 4, 8, 8
GROUP = 32
SHARE = 16
ROWS = 104


def kernel(image_total, idx_ref, feat_ref, factor_ref, mean_ref,
           idx_pad, feat, wide, sbuf, rbuf, pbuf, r2buf, lbuf, r3buf,
           load_sem, send1, recv1, send2, recv2, send3, recv3):
    batches, imgs, width, positions = feat_ref.shape
    images = batches * imgs
    keep = idx_ref.shape[1]
    grp = lax.axis_index("grp")
    pos = lax.axis_index("pos")
    y, x_hi = grp // 2, grp % 2
    x_lo, z, core = pos // (2 * NZ), (pos // 2) % NZ, pos % 2
    x = 2 * x_hi + x_lo
    y_hi, y_lo = y // 2, y % 2
    z_hi, z_lo = z // 2, z % 2

    def device(xx, yy, zz, cc):
        return {"grp": yy * 2 + xx // 2, "pos": ((xx % 2) * NZ + zz) * 2 + cc}

    def partner1(t):
        xx = (x + t // 8) % 4
        zl = (z_lo + (t // 4) % 2) % 2
        yl = (y_lo + (t // 2) % 2) % 2
        cc = (core + t % 2) % 2
        return ((xx * 2 + zl) * 2 + yl) * 2 + cc, device(xx, 2 * y_hi + yl, 2 * z_hi + zl, cc)

    def partner2(t):
        q = (z_hi * 4 + y_hi + t) % 16
        return q, device(x, 2 * (q % 4) + y_lo, 2 * (q // 4) + z_lo, core)

    def partner3(t):
        o = (own + t) % 16
        xh, yl, yh = o // 8, (o // 4) % 2, o % 4
        return o, device(2 * xh + x_lo, 2 * yh + yl, z, core)

    me = ((x * 2 + z_lo) * 2 + y_lo) * 2 + core
    mine = z_hi * 4 + y_hi
    own = x_hi * 8 + y_lo * 4 + y_hi

    copies = []
    for b in range(batches):
        for i in range(imgs):
            k = b * imgs + i
            c = pltpu.make_async_copy(feat_ref.at[b, i], feat.at[k], load_sem.at[k])
            c.start()
            copies.append(c)

    barrier = pltpu.get_barrier_semaphore()

    def greet(partner):
        def body(t, carry):
            pl.semaphore_signal(barrier, inc=1, device_id=partner(t)[1], device_id_type=pl.DeviceIdType.MESH)
            return carry
        return body

    lax.fori_loop(1, GROUP, greet(partner1), 0)
    lax.fori_loop(1, 16, greet(partner2), 0)
    lax.fori_loop(1, 16, greet(partner3), 0)

    idx_pad[...] = jnp.full(idx_pad.shape, -1, jnp.int32)
    idx_pad[0:1, 0:keep] = idx_ref[...]
    selector = jnp.where(
        lax.broadcasted_iota(jnp.int32, (4 * LANES, LANES), 0) == idx_pad[0:1, :], 1.0, 0.0
    ).T[:, :width].astype(jnp.bfloat16)
    for k in range(images):
        copies[k].wait()
        picked = jnp.dot(selector, feat[k], preferred_element_type=jnp.float32)
        wide[pl.ds(k, positions, stride=images), :] = picked.T
    chunk = 4 * images
    ones_lane = lax.broadcasted_iota(jnp.int32, (chunk, LANES), 1) == keep
    for d in range(GROUP):
        xx, zl, yl, cc = d // 8, (d // 4) % 2, (d // 2) % 2, d % 2
        for zh in range(4):
            first = 16 * (((xx % 2) * NZ + 2 * zh + zl) * 2 + cc) + 8 * (xx // 2) + 4 * yl
            piece = wide[first * images:first * images + chunk, :]
            sbuf[d, zh * chunk:(zh + 1) * chunk, :] = jnp.where(ones_lane, 1.0, piece).astype(jnp.bfloat16)

    pl.semaphore_wait(barrier, GROUP - 1 + 15 + 15)

    def copy1(t):
        d, dev = partner1(t)
        return pltpu.make_async_remote_copy(
            src_ref=sbuf.at[d], dst_ref=rbuf.at[me], send_sem=send1.at[t], recv_sem=recv1.at[me],
            device_id=dev, device_id_type=pl.DeviceIdType.MESH)

    def got1(t):
        s, dev = partner1(t)
        return pltpu.make_async_remote_copy(
            src_ref=sbuf.at[s], dst_ref=rbuf.at[s], send_sem=send1.at[t], recv_sem=recv1.at[s],
            device_id=dev, device_id_type=pl.DeviceIdType.MESH)

    def loop(lo, hi, act):
        def body(t, carry):
            act(t)
            return carry
        lax.fori_loop(lo, hi, body, 0)

    loop(1, GROUP, lambda t: copy1(t).start())
    rbuf[me] = sbuf[me]
    loop(1, GROUP, lambda t: got1(t).wait_recv())

    half = (lax.broadcasted_iota(jnp.int32, (16, LANES), 0) < images).astype(jnp.float32)
    even = half.astype(jnp.bfloat16)
    odd = (1.0 - half).astype(jnp.bfloat16)

    def pair(j, carry):
        tile = rbuf[:, pl.ds(pl.multiple_of(16 * j, 16), 16), :]
        flat = tile.reshape(GROUP * 16, LANES)
        rhs = jnp.concatenate(
            [(tile * even[None]).reshape(GROUP * 16, LANES), (tile * odd[None]).reshape(GROUP * 16, LANES)], axis=1)
        both = lax.dot_general(flat, rhs, (((0,), (0,)), ((), ())), preferred_element_type=jnp.float32)
        pbuf[2 * j] = both[:ROWS, :LANES]
        pbuf[2 * j + 1] = both[:ROWS, LANES:]
        return carry

    lax.fori_loop(0, SHARE // 2, pair, 0)

    def copy2(t):
        q, dev = partner2(t)
        return pltpu.make_async_remote_copy(
            src_ref=pbuf.at[q], dst_ref=r2buf.at[mine], send_sem=send2.at[t], recv_sem=recv2.at[mine],
            device_id=dev, device_id_type=pl.DeviceIdType.MESH)

    def got2(t):
        s, dev = partner2(t)
        return pltpu.make_async_remote_copy(
            src_ref=pbuf.at[s], dst_ref=r2buf.at[s], send_sem=send2.at[t], recv_sem=recv2.at[s],
            device_id=dev, device_id_type=pl.DeviceIdType.MESH)

    loop(1, 16, lambda t: copy2(t).start())
    r2buf[mine] = pbuf[mine]
    loop(1, 16, lambda t: got2(t).wait_recv())
    total = jnp.sum(r2buf[...], axis=0)

    row = lax.broadcasted_iota(jnp.int32, (ROWS, LANES), 0)
    lane = lax.broadcasted_iota(jnp.int32, (ROWS, LANES), 1)
    mean_row = total[keep:keep + 1, :] / image_total
    mean_col = total[:, keep:keep + 1] / image_total
    cov = (total - (image_total * mean_col) * mean_row) / (image_total - 1)
    cov = cov + jnp.where(row == lane, RIDGE, 0.0)
    cov = jnp.where((row < keep) & (lane < keep), cov, jnp.where(row == lane, 1.0, 0.0))
    blocks = [cov[8 * i:8 * i + 8, :] for i in range(ROWS // 8)]
    sub = lax.broadcasted_iota(jnp.int32, (8, LANES), 0)

    def spread_row(v, k):
        return jnp.broadcast_to(v[k:k + 1, :], (8, LANES))

    upper = []
    count = ROWS // 8
    for j in range(count):
        cols = [[jnp.broadcast_to(blocks[i][:, 8 * j + k:8 * j + k + 1], (8, LANES)) for k in range(8)]
                for i in range(j, count)]
        root = jnp.zeros((8, LANES), jnp.float32)
        for k in range(8):
            pivot = spread_row(cols[0][k], k)
            inv = 1.0 / pivot
            root = jnp.where(sub == k, lax.rsqrt(pivot), root)
            main_row = spread_row(blocks[j], k) * inv
            col_rows = [spread_row(cols[0][m], k) * inv for m in range(k + 1, 8)]
            for i in range(j, count):
                left = cols[i - j][k]
                if i == j:
                    left = jnp.where(sub > k, left, 0.0)
                blocks[i] = blocks[i] - left * main_row
                for m in range(k + 1, 8):
                    cols[i - j][m] = cols[i - j][m] - left * col_rows[m - k - 1]
        upper.append(blocks[j] * root)
    full = jnp.concatenate(upper + [jnp.zeros((LANES - ROWS, LANES), jnp.float32)], axis=0)
    row128 = lax.broadcasted_iota(jnp.int32, (LANES, LANES), 0)
    lane128 = lax.broadcasted_iota(jnp.int32, (LANES, LANES), 1)
    full = jnp.where(lane128 >= row128, full, 0.0)
    lower = full.T
    lower = jnp.where(row128 < keep, lower, jnp.where(row128 == keep, mean_row, 0.0))
    lbuf[...] = lower[:ROWS, :]

    def copy3(t):
        o, dev = partner3(t)
        return pltpu.make_async_remote_copy(
            src_ref=lbuf, dst_ref=r3buf.at[own], send_sem=send3.at[t], recv_sem=recv3.at[own],
            device_id=dev, device_id_type=pl.DeviceIdType.MESH)

    def got3(t):
        s, dev = partner3(t)
        return pltpu.make_async_remote_copy(
            src_ref=lbuf, dst_ref=r3buf.at[s], send_sem=send3.at[t], recv_sem=recv3.at[s],
            device_id=dev, device_id_type=pl.DeviceIdType.MESH)

    loop(1, 16, lambda t: copy3(t).start())
    r3buf[own] = lbuf[...]
    loop(1, 16, lambda t: got3(t).wait_recv())
    for o in range(16):
        factor_ref[:, o, :] = r3buf[o, :keep, :keep]
        mean_ref[o:o + 1, :] = r3buf[o, keep:keep + 1, :keep]

    loop(1, GROUP, lambda t: copy1(t).wait_send())
    loop(1, 16, lambda t: copy2(t).wait_send())
    loop(1, 16, lambda t: copy3(t).wait_send())


def local(features, channel_index):
    batches, imgs, positions, width = features.shape
    keep = channel_index.shape[0]
    images = batches * imgs
    image_total = images * lax.axis_size("pos") * lax.axis_size("grp")
    owned = positions // lax.axis_size("pos")
    f32, bf16 = jnp.float32, jnp.bfloat16
    vmem = pl.BlockSpec(memory_space=pltpu.VMEM)
    factor, mean_vec = pl.pallas_call(
        lambda *refs: kernel(image_total, *refs),
        out_shape=(jax.ShapeDtypeStruct((keep, owned, keep), f32), jax.ShapeDtypeStruct((owned, keep), f32)),
        in_specs=[vmem, pl.BlockSpec(memory_space=pl.ANY)],
        out_specs=(vmem, vmem),
        scratch_shapes=[
            pltpu.VMEM((8, LANES), jnp.int32),
            pltpu.VMEM((images, width, positions), bf16),
            pltpu.VMEM((images * positions, LANES), f32),
            pltpu.VMEM((GROUP, SHARE * images, LANES), bf16),
            pltpu.VMEM((GROUP, SHARE * images, LANES), bf16),
            pltpu.VMEM((SHARE, ROWS, LANES), f32),
            pltpu.VMEM((SHARE, ROWS, LANES), f32),
            pltpu.VMEM((ROWS, LANES), f32),
            pltpu.VMEM((SHARE, ROWS, LANES), f32),
            pltpu.SemaphoreType.DMA((images,)),
            pltpu.SemaphoreType.DMA((GROUP,)),
            pltpu.SemaphoreType.DMA((GROUP,)),
            pltpu.SemaphoreType.DMA((16,)),
            pltpu.SemaphoreType.DMA((16,)),
            pltpu.SemaphoreType.DMA((16,)),
            pltpu.SemaphoreType.DMA((16,)),
        ],
        compiler_params=pltpu.CompilerParams(
            collective_id=0, has_side_effects=True, vmem_limit_bytes=60 * 1024 * 1024),
        name="gaussian_stats",
    )(channel_index.reshape(1, keep), jnp.swapaxes(features, 2, 3))
    return jnp.swapaxes(factor, 0, 1), mean_vec


def solution(mesh):
    return jax.shard_map(
        local,
        mesh=mesh,
        in_specs=(P(None, ("grp", "pos"), None, None), P()),
        out_specs=(P("pos", None, None), P("pos", None)),
        check_vma=False,
    )
```

```python
import jax
import jax.numpy as jnp
from jax import lax
from jax.experimental import pallas as pl
from jax.experimental.pallas import tpu as pltpu
from jax.sharding import PartitionSpec as P

RIDGE = 0.01
LANES = 128
NX, NY, NZ = 4, 8, 8
GROUP = 32
SHARE = 16
ROWS = 104
HEAD, PACK = 56, 48


def lanes_of(rows):
    return lax.broadcasted_iota(jnp.int32, (rows, LANES), 1)


def rows_of(rows):
    return lax.broadcasted_iota(jnp.int32, (rows, LANES), 0)


def pack(low, up):
    row, lane = rows_of(PACK), lanes_of(PACK)
    corner = pltpu.roll(up[PACK:HEAD, :], 116 - PACK, 1)
    lane8 = lanes_of(8)
    out = jnp.where(lane <= HEAD + row, low[HEAD:ROWS, :], pltpu.roll(up[:PACK, :], HEAD + 1, 1))
    first = jnp.where((lane8 >= 116) & (lane8 < 124), corner, out[:8, :])
    return jnp.concatenate([first, out[8:, :]], axis=0)


def unpack_head(packed):
    head = jnp.concatenate(
        [pltpu.roll(packed, LANES - HEAD - 1, 1), pltpu.roll(packed[:8, :], LANES - 116 + PACK, 1)], axis=0)
    lane = lanes_of(HEAD)
    return jnp.where((lane >= rows_of(HEAD)) & (lane < HEAD), head, 0.0)


def unpack_tail(packed):
    return jnp.where(lanes_of(PACK) <= HEAD + rows_of(PACK), packed, 0.0)


def kernel(image_total, idx_ref, feat_ref, factor_ref, mean_ref,
           idx_pad, feat, wide, sbuf, rbuf, pbuf, r2buf, lbuf, r3buf,
           load_sem, send1, recv1, send2, recv2, send3, recv3):
    batches, imgs, width, positions = feat_ref.shape
    images = batches * imgs
    keep = idx_ref.shape[1]
    grp = lax.axis_index("grp")
    pos = lax.axis_index("pos")
    y, x_hi = grp // 2, grp % 2
    x_lo, z, core = pos // (2 * NZ), (pos // 2) % NZ, pos % 2
    x = 2 * x_hi + x_lo
    y_hi, y_lo = y // 2, y % 2
    z_hi, z_lo = z // 2, z % 2

    def device(xx, yy, zz, cc):
        return {"grp": yy * 2 + xx // 2, "pos": ((xx % 2) * NZ + zz) * 2 + cc}

    def partner1(t):
        xx = (x + t // 8) % 4
        zl = (z_lo + (t // 4) % 2) % 2
        yl = (y_lo + (t // 2) % 2) % 2
        cc = (core + t % 2) % 2
        return ((xx * 2 + zl) * 2 + yl) * 2 + cc, device(xx, 2 * y_hi + yl, 2 * z_hi + zl, cc)

    def partner2(t):
        q = (z_hi * 4 + y_hi + t) % 16
        return q, device(x, 2 * (q % 4) + y_lo, 2 * (q // 4) + z_lo, core)

    def partner3(t):
        o = (own + t) % 16
        xh, yl, yh = o // 8, (o // 4) % 2, o % 4
        return o, device(2 * xh + x_lo, 2 * yh + yl, z, core)

    me = ((x * 2 + z_lo) * 2 + y_lo) * 2 + core
    mine = z_hi * 4 + y_hi
    own = x_hi * 8 + y_lo * 4 + y_hi

    copies = []
    for b in range(batches):
        for i in range(imgs):
            k = b * imgs + i
            c = pltpu.make_async_copy(feat_ref.at[b, i], feat.at[k], load_sem.at[k])
            c.start()
            copies.append(c)

    barrier = pltpu.get_barrier_semaphore()

    def greet(partner):
        def body(t, carry):
            pl.semaphore_signal(barrier, inc=1, device_id=partner(t)[1], device_id_type=pl.DeviceIdType.MESH)
            return carry
        return body

    lax.fori_loop(1, GROUP, greet(partner1), 0)
    lax.fori_loop(1, 16, greet(partner2), 0)
    lax.fori_loop(1, 16, greet(partner3), 0)

    idx_pad[...] = jnp.full(idx_pad.shape, -1, jnp.int32)
    idx_pad[0:1, 0:keep] = idx_ref[...]
    selector = jnp.where(
        lax.broadcasted_iota(jnp.int32, (4 * LANES, LANES), 0) == idx_pad[0:1, :], 1.0, 0.0
    ).T[:, :width].astype(jnp.bfloat16)
    for k in range(images):
        copies[k].wait()
        picked = jnp.dot(selector, feat[k], preferred_element_type=jnp.float32)
        wide[pl.ds(k, positions, stride=images), :] = picked.T
    chunk = 4 * images
    ones_lane = lax.broadcasted_iota(jnp.int32, (chunk, LANES), 1) == keep
    for d in range(GROUP):
        xx, zl, yl, cc = d // 8, (d // 4) % 2, (d // 2) % 2, d % 2
        for zh in range(4):
            first = 16 * (((xx % 2) * NZ + 2 * zh + zl) * 2 + cc) + 8 * (xx // 2) + 4 * yl
            piece = wide[first * images:first * images + chunk, :]
            sbuf[d, zh * chunk:(zh + 1) * chunk, :] = jnp.where(ones_lane, 1.0, piece).astype(jnp.bfloat16)

    pl.semaphore_wait(barrier, GROUP - 1 + 15 + 15)

    def copy1(t):
        d, dev = partner1(t)
        return pltpu.make_async_remote_copy(
            src_ref=sbuf.at[d], dst_ref=rbuf.at[me], send_sem=send1.at[t], recv_sem=recv1.at[me],
            device_id=dev, device_id_type=pl.DeviceIdType.MESH)

    def got1(t):
        s, dev = partner1(t)
        return pltpu.make_async_remote_copy(
            src_ref=sbuf.at[s], dst_ref=rbuf.at[s], send_sem=send1.at[t], recv_sem=recv1.at[s],
            device_id=dev, device_id_type=pl.DeviceIdType.MESH)

    def loop(lo, hi, act):
        def body(t, carry):
            act(t)
            return carry
        lax.fori_loop(lo, hi, body, 0)

    loop(1, GROUP, lambda t: copy1(t).start())
    rbuf[me] = sbuf[me]
    loop(1, GROUP, lambda t: got1(t).wait_recv())

    half = (lax.broadcasted_iota(jnp.int32, (16, LANES), 0) < images).astype(jnp.float32)
    even = half.astype(jnp.bfloat16)
    odd = (1.0 - half).astype(jnp.bfloat16)

    def pair(j, carry):
        tile = rbuf[:, pl.ds(pl.multiple_of(16 * j, 16), 16), :]
        flat = tile.reshape(GROUP * 16, LANES)
        rhs = jnp.concatenate(
            [(tile * even[None]).reshape(GROUP * 16, LANES), (tile * odd[None]).reshape(GROUP * 16, LANES)], axis=1)
        both = lax.dot_general(flat, rhs, (((0,), (0,)), ((), ())), preferred_element_type=jnp.float32)
        pbuf[2 * j] = pack(both[:, :LANES], both[:, :LANES])
        pbuf[2 * j + 1] = pack(both[:, LANES:], both[:, LANES:])
        return carry

    lax.fori_loop(0, SHARE // 2, pair, 0)

    def copy2(t):
        q, dev = partner2(t)
        return pltpu.make_async_remote_copy(
            src_ref=pbuf.at[q], dst_ref=r2buf.at[mine], send_sem=send2.at[t], recv_sem=recv2.at[mine],
            device_id=dev, device_id_type=pl.DeviceIdType.MESH)

    def got2(t):
        s, dev = partner2(t)
        return pltpu.make_async_remote_copy(
            src_ref=pbuf.at[s], dst_ref=r2buf.at[s], send_sem=send2.at[t], recv_sem=recv2.at[s],
            device_id=dev, device_id_type=pl.DeviceIdType.MESH)

    loop(1, 16, lambda t: copy2(t).start())
    r2buf[mine] = pbuf[mine]
    loop(1, 16, lambda t: got2(t).wait_recv())
    packed = jnp.sum(r2buf[...], axis=0)
    half_total = jnp.concatenate(
        [unpack_head(packed), unpack_tail(packed), jnp.zeros((LANES - ROWS, LANES), jnp.float32)], axis=0)
    row128, lane128 = rows_of(LANES), lanes_of(LANES)
    total = (half_total + jnp.where(row128 == lane128, 0.0, half_total.T))[:ROWS, :]

    row = lax.broadcasted_iota(jnp.int32, (ROWS, LANES), 0)
    lane = lax.broadcasted_iota(jnp.int32, (ROWS, LANES), 1)
    mean_row = total[keep:keep + 1, :] / image_total
    mean_col = total[:, keep:keep + 1] / image_total
    cov = (total - (image_total * mean_col) * mean_row) / (image_total - 1)
    cov = cov + jnp.where(row == lane, RIDGE, 0.0)
    cov = jnp.where((row < keep) & (lane < keep), cov, jnp.where(row == lane, 1.0, 0.0))
    blocks = [cov[8 * i:8 * i + 8, :] for i in range(ROWS // 8)]
    sub = lax.broadcasted_iota(jnp.int32, (8, LANES), 0)

    def spread_row(v, k):
        return jnp.broadcast_to(v[k:k + 1, :], (8, LANES))

    upper = []
    count = ROWS // 8
    for j in range(count):
        cols = [[jnp.broadcast_to(blocks[i][:, 8 * j + k:8 * j + k + 1], (8, LANES)) for k in range(8)]
                for i in range(j, count)]
        root = jnp.zeros((8, LANES), jnp.float32)
        for k in range(8):
            pivot = spread_row(cols[0][k], k)
            inv = 1.0 / pivot
            root = jnp.where(sub == k, lax.rsqrt(pivot), root)
            main_row = spread_row(blocks[j], k) * inv
            col_rows = [spread_row(cols[0][m], k) * inv for m in range(k + 1, 8)]
            for i in range(j, count):
                left = cols[i - j][k]
                if i == j:
                    left = jnp.where(sub > k, left, 0.0)
                blocks[i] = blocks[i] - left * main_row
                for m in range(k + 1, 8):
                    cols[i - j][m] = cols[i - j][m] - left * col_rows[m - k - 1]
        upper.append(blocks[j] * root)
    full = jnp.concatenate(upper + [jnp.zeros((LANES - ROWS, LANES), jnp.float32)], axis=0)
    full = jnp.where(lane128 >= row128, full, 0.0)
    lower = full.T
    out = pack(lower, full)
    lane48 = lanes_of(PACK)
    means = jnp.where(lane48 == 113, mean_col[:PACK], mean_col[PACK:2 * PACK])
    lbuf[...] = jnp.where((lane48 == 113) | (lane48 == 114), means, out)
    lbuf[:8, :] = jnp.where(lanes_of(8) == 115, mean_col[2 * PACK:], lbuf[:8, :])

    def copy3(t):
        o, dev = partner3(t)
        return pltpu.make_async_remote_copy(
            src_ref=lbuf, dst_ref=r3buf.at[own], send_sem=send3.at[t], recv_sem=recv3.at[own],
            device_id=dev, device_id_type=pl.DeviceIdType.MESH)

    def got3(t):
        s, dev = partner3(t)
        return pltpu.make_async_remote_copy(
            src_ref=lbuf, dst_ref=r3buf.at[s], send_sem=send3.at[t], recv_sem=recv3.at[s],
            device_id=dev, device_id_type=pl.DeviceIdType.MESH)

    loop(1, 16, lambda t: copy3(t).start())
    r3buf[own] = lbuf[...]
    loop(1, 16, lambda t: got3(t).wait_recv())
    for o in range(0, 16, 2):
        turned = []
        for i in range(2):
            mine3 = r3buf[o + i]
            turn = pltpu.roll(mine3, LANES - HEAD - 1, 1)
            extra = pltpu.roll(mine3[:8, :], LANES - 116 + PACK, 1)
            lane = lanes_of(PACK)
            turn = jnp.where((lane >= rows_of(PACK)) & (lane < HEAD + 3), turn, 0.0)
            lane8 = lanes_of(8)
            extra = jnp.where((lane8 >= PACK + rows_of(8)) & (lane8 < HEAD), extra, 0.0)
            turned.append(jnp.concatenate([turn, extra, jnp.zeros((8, LANES), jnp.float32)], axis=0))
        both = (turned[0] + pltpu.roll(turned[1], 64, 1)).T
        for i in range(2):
            head = both[64 * i:64 * i + 64, :]
            factor_ref[0:HEAD, o + i, 0:64] = head[:HEAD, :]
            factor_ref[0:HEAD, o + i, 64:keep] = jnp.zeros((HEAD, keep - 64), jnp.float32)
            factor_ref[HEAD:keep, o + i, :] = unpack_tail(r3buf[o + i])[:keep - HEAD, :keep]
            mean_ref[o + i:o + i + 1, 0:PACK] = head[HEAD:HEAD + 1, :PACK]
            mean_ref[o + i:o + i + 1, PACK:2 * PACK] = head[HEAD + 1:HEAD + 2, :PACK]
            mean_ref[o + i:o + i + 1, 2 * PACK:keep] = head[HEAD + 2:HEAD + 3, :keep - 2 * PACK]

    loop(1, GROUP, lambda t: copy1(t).wait_send())
    loop(1, 16, lambda t: copy2(t).wait_send())
    loop(1, 16, lambda t: copy3(t).wait_send())


def local(features, channel_index):
    batches, imgs, positions, width = features.shape
    keep = channel_index.shape[0]
    images = batches * imgs
    image_total = images * lax.axis_size("pos") * lax.axis_size("grp")
    owned = positions // lax.axis_size("pos")
    f32, bf16 = jnp.float32, jnp.bfloat16
    vmem = pl.BlockSpec(memory_space=pltpu.VMEM)
    factor, mean_vec = pl.pallas_call(
        lambda *refs: kernel(image_total, *refs),
        out_shape=(jax.ShapeDtypeStruct((keep, owned, keep), f32), jax.ShapeDtypeStruct((owned, keep), f32)),
        in_specs=[vmem, pl.BlockSpec(memory_space=pl.ANY)],
        out_specs=(vmem, vmem),
        scratch_shapes=[
            pltpu.VMEM((8, LANES), jnp.int32),
            pltpu.VMEM((images, width, positions), bf16),
            pltpu.VMEM((images * positions, LANES), f32),
            pltpu.VMEM((GROUP, SHARE * images, LANES), bf16),
            pltpu.VMEM((GROUP, SHARE * images, LANES), bf16),
            pltpu.VMEM((SHARE, PACK, LANES), f32),
            pltpu.VMEM((SHARE, PACK, LANES), f32),
            pltpu.VMEM((PACK, LANES), f32),
            pltpu.VMEM((SHARE, PACK, LANES), f32),
            pltpu.SemaphoreType.DMA((images,)),
            pltpu.SemaphoreType.DMA((GROUP,)),
            pltpu.SemaphoreType.DMA((GROUP,)),
            pltpu.SemaphoreType.DMA((16,)),
            pltpu.SemaphoreType.DMA((16,)),
            pltpu.SemaphoreType.DMA((16,)),
            pltpu.SemaphoreType.DMA((16,)),
        ],
        compiler_params=pltpu.CompilerParams(
            collective_id=0, has_side_effects=True, vmem_limit_bytes=60 * 1024 * 1024),
        name="gaussian_stats",
    )(channel_index.reshape(1, keep), jnp.swapaxes(features, 2, 3))
    return jnp.swapaxes(factor, 0, 1), mean_vec


def solution(mesh):
    return jax.shard_map(
        local,
        mesh=mesh,
        in_specs=(P(None, ("grp", "pos"), None, None), P()),
        out_specs=(P("pos", None, None), P("pos", None)),
        check_vma=False,
    )
```

```python
import jax
import jax.numpy as jnp
from jax import lax
from jax.experimental import pallas as pl
from jax.experimental.pallas import tpu as pltpu
from jax.sharding import PartitionSpec as P

RIDGE = 0.01
LANES = 128
NX, NY, NZ = 4, 8, 8
GROUP = 32
SHARE = 16
ROWS = 104
HEAD, PACK = 56, 48


def lanes_of(rows):
    return lax.broadcasted_iota(jnp.int32, (rows, LANES), 1)


def rows_of(rows):
    return lax.broadcasted_iota(jnp.int32, (rows, LANES), 0)


def pack(low, up):
    row, lane = rows_of(PACK), lanes_of(PACK)
    corner = pltpu.roll(up[PACK:HEAD, :], 116 - PACK, 1)
    lane8 = lanes_of(8)
    out = jnp.where(lane <= HEAD + row, low[HEAD:ROWS, :], pltpu.roll(up[:PACK, :], HEAD + 1, 1))
    first = jnp.where((lane8 >= 116) & (lane8 < 124), corner, out[:8, :])
    return jnp.concatenate([first, out[8:, :]], axis=0)


def unpack_head(packed):
    head = jnp.concatenate(
        [pltpu.roll(packed, LANES - HEAD - 1, 1), pltpu.roll(packed[:8, :], LANES - 116 + PACK, 1)], axis=0)
    lane = lanes_of(HEAD)
    return jnp.where((lane >= rows_of(HEAD)) & (lane < HEAD), head, 0.0)


def unpack_tail(packed):
    return jnp.where(lanes_of(PACK) <= HEAD + rows_of(PACK), packed, 0.0)


def ring(d, n):
    return min(d, n - d)


ORDER1 = sorted(range(1, GROUP), key=lambda t: -(ring(t // 8, 4) + (t // 4) % 2 + (t // 2) % 2))
ORDER3 = sorted(range(1, 8), key=lambda t: -ring(t, 8))
ORDER2 = sorted(range(1, 16), key=lambda t: -2 * (ring(t // 4, 4) + ring(t % 4, 4)))


def kernel(image_total, idx_ref, feat_ref, r3buf,
           idx, idx_pad, feat, wide, sbuf, rbuf, pbuf, r2buf, lbuf,
           idx_sem, load_sem, send1, recv1, send2, recv2, send3, recv3):
    batches, imgs, width, positions = feat_ref.shape
    images = batches * imgs
    keep = idx_ref.shape[1]
    grp = lax.axis_index("grp")
    pos = lax.axis_index("pos")
    y, x_hi = grp // 2, grp % 2
    x_lo, z, core = pos // (2 * NZ), (pos // 2) % NZ, pos % 2
    x = 2 * x_hi + x_lo
    y_hi, y_lo = y // 2, y % 2
    z_hi, z_lo = z // 2, z % 2

    def device(xx, yy, zz, cc):
        return {"grp": yy * 2 + xx // 2, "pos": ((xx % 2) * NZ + zz) * 2 + cc}

    def partner1(t):
        xx = (x + t // 8) % 4
        zl = (z_lo + (t // 4) % 2) % 2
        yl = (y_lo + (t // 2) % 2) % 2
        cc = (core + t % 2) % 2
        return ((xx * 2 + zl) * 2 + yl) * 2 + cc, device(xx, 2 * y_hi + yl, 2 * z_hi + zl, cc)

    def partner2(t):
        q = ((z_hi + t // 4) % 4) * 4 + (y_hi + t % 4) % 4
        return q, device(x, 2 * (q % 4) + y_lo, 2 * (q // 4) + z_lo, core)

    def place(xh, yy):
        return xh * 8 + (yy % 2) * 4 + yy // 2

    def partner3(t):
        yy = (y + t) % 8
        return place(x_hi, yy), device(x, yy, z, core)

    across = device((x + 2) % 4, y, z, core)

    me = ((x * 2 + z_lo) * 2 + y_lo) * 2 + core
    mine = z_hi * 4 + y_hi
    own = x_hi * 8 + y_lo * 4 + y_hi

    idx_copy = pltpu.make_async_copy(idx_ref, idx, idx_sem)
    idx_copy.start()
    copies = []
    for b in range(batches):
        for i in range(imgs):
            k = b * imgs + i
            c = pltpu.make_async_copy(feat_ref.at[b, i], feat.at[k], load_sem.at[k])
            c.start()
            copies.append(c)

    barrier = pltpu.get_barrier_semaphore()

    greetings = [partner2(t)[1] for t in ORDER2] + [partner1(t)[1] for t in ORDER1]

    def greet(devices):
        for dev in devices:
            pl.semaphore_signal(barrier, inc=1, device_id=dev, device_id_type=pl.DeviceIdType.MESH)

    greet(greetings)

    idx_pad[...] = jnp.full(idx_pad.shape, -1, jnp.int32)
    idx_copy.wait()
    idx_pad[0:1, 0:keep] = idx[...]
    selector = jnp.where(
        lax.broadcasted_iota(jnp.int32, (4 * LANES, LANES), 0) == idx_pad[0:1, :], 1.0, 0.0
    ).T[:, :width].astype(jnp.bfloat16)
    for k in range(images):
        copies[k].wait()
        picked = jnp.dot(selector, feat[k], preferred_element_type=jnp.float32)
        wide[pl.ds(k, positions, stride=images), :] = picked.T
    chunk = 4 * images
    ones_lane = lax.broadcasted_iota(jnp.int32, (chunk, LANES), 1) == keep
    for d in range(GROUP):
        xx, zl, yl, cc = d // 8, (d // 4) % 2, (d // 2) % 2, d % 2
        for zh in range(4):
            first = 16 * (((xx % 2) * NZ + 2 * zh + zl) * 2 + cc) + 8 * (xx // 2) + 4 * yl
            piece = wide[first * images:first * images + chunk, :]
            sbuf[d, zh * chunk:(zh + 1) * chunk, :] = jnp.where(ones_lane, 1.0, piece).astype(jnp.bfloat16)

    pl.semaphore_wait(barrier, GROUP - 1 + 15)

    def copy1(t):
        d, dev = partner1(t)
        return pltpu.make_async_remote_copy(
            src_ref=sbuf.at[d], dst_ref=rbuf.at[me], send_sem=send1.at[t], recv_sem=recv1.at[me],
            device_id=dev, device_id_type=pl.DeviceIdType.MESH)

    def got1(t):
        s, dev = partner1(t)
        return pltpu.make_async_remote_copy(
            src_ref=sbuf.at[s], dst_ref=rbuf.at[s], send_sem=send1.at[t], recv_sem=recv1.at[s],
            device_id=dev, device_id_type=pl.DeviceIdType.MESH)

    def loop(lo, hi, act):
        def body(t, carry):
            act(t)
            return carry
        lax.fori_loop(lo, hi, body, 0)

    for t in ORDER1:
        copy1(t).start()
    rbuf[me] = sbuf[me]
    loop(1, GROUP, lambda t: got1(t).wait_recv())

    half = (lax.broadcasted_iota(jnp.int32, (16, LANES), 0) < images).astype(jnp.float32)
    even = half.astype(jnp.bfloat16)
    odd = (1.0 - half).astype(jnp.bfloat16)

    def copy2(q, n):
        dev = device(x, 2 * (q % 4) + y_lo, 2 * (q // 4) + z_lo, core)
        return pltpu.make_async_remote_copy(
            src_ref=pbuf.at[q], dst_ref=r2buf.at[mine], send_sem=send2.at[n], recv_sem=recv2.at[mine],
            device_id=dev, device_id_type=pl.DeviceIdType.MESH)

    sent2 = []
    for dz, dy in ((2, 1), (2, 0), (1, 1), (3, 1), (1, 0), (3, 0), (0, 1), (0, 0)):
        j = ((z_hi + dz) % 4) * 2 + (y_hi // 2 + dy) % 2
        tile = rbuf[:, pl.ds(pl.multiple_of(16 * j, 16), 16), :]
        flat = tile.reshape(GROUP * 16, LANES)
        rhs = jnp.concatenate(
            [(tile * even[None]).reshape(GROUP * 16, LANES), (tile * odd[None]).reshape(GROUP * 16, LANES)], axis=1)
        both = lax.dot_general(flat, rhs, (((0,), (0,)), ((), ())), preferred_element_type=jnp.float32)
        pbuf[2 * j] = pack(both[:, :LANES], both[:, :LANES])
        pbuf[2 * j + 1] = pack(both[:, LANES:], both[:, LANES:])
        for q in ([2 * j, 2 * j + 1] if dz or dy else [2 * j + 1 - y_hi % 2]):
            copy = copy2(q, len(sent2))
            copy.start()
            sent2.append(copy)

    def got2(t):
        s, dev = partner2(t)
        return pltpu.make_async_remote_copy(
            src_ref=pbuf.at[s], dst_ref=r2buf.at[s], send_sem=send2.at[t], recv_sem=recv2.at[s],
            device_id=dev, device_id_type=pl.DeviceIdType.MESH)

    r2buf[mine] = pbuf[mine]
    loop(1, 16, lambda t: got2(t).wait_recv())
    packed = jnp.sum(r2buf[...], axis=0)
    half_total = jnp.concatenate(
        [unpack_head(packed), unpack_tail(packed), jnp.zeros((LANES - ROWS, LANES), jnp.float32)], axis=0)
    row128, lane128 = rows_of(LANES), lanes_of(LANES)
    total = (half_total + jnp.where(row128 == lane128, 0.0, half_total.T))[:ROWS, :]

    row = lax.broadcasted_iota(jnp.int32, (ROWS, LANES), 0)
    lane = lax.broadcasted_iota(jnp.int32, (ROWS, LANES), 1)
    mean_row = total[keep:keep + 1, :] / image_total
    mean_col = total[:, keep:keep + 1] / image_total
    cov = (total - (image_total * mean_col) * mean_row) / (image_total - 1)
    cov = cov + jnp.where(row == lane, RIDGE, 0.0)
    cov = jnp.where((row < keep) & (lane < keep), cov, jnp.where(row == lane, 1.0, 0.0))
    blocks = [cov[8 * i:8 * i + 8, :] for i in range(ROWS // 8)]
    sub = lax.broadcasted_iota(jnp.int32, (8, LANES), 0)

    def spread_row(v, k):
        return jnp.broadcast_to(v[k:k + 1, :], (8, LANES))

    upper = []
    count = ROWS // 8
    for j in range(count):
        cols = [[jnp.broadcast_to(blocks[i][:, 8 * j + k:8 * j + k + 1], (8, LANES)) for k in range(8)]
                for i in range(j, count)]
        root = jnp.zeros((8, LANES), jnp.float32)
        for k in range(8):
            pivot = spread_row(cols[0][k], k)
            inv = 1.0 / pivot
            root = jnp.where(sub == k, lax.rsqrt(pivot), root)
            main_row = spread_row(blocks[j], k) * inv
            col_rows = [spread_row(cols[0][m], k) * inv for m in range(k + 1, 8)]
            for i in range(j, count):
                left = cols[i - j][k]
                if i == j:
                    left = jnp.where(sub > k, left, 0.0)
                blocks[i] = blocks[i] - left * main_row
                for m in range(k + 1, 8):
                    cols[i - j][m] = cols[i - j][m] - left * col_rows[m - k - 1]
        upper.append(blocks[j] * root)
    full = jnp.concatenate(upper + [jnp.zeros((LANES - ROWS, LANES), jnp.float32)], axis=0)
    full = jnp.where(lane128 >= row128, full, 0.0)
    lower = full.T
    out = pack(lower, full)
    lane48 = lanes_of(PACK)
    means = jnp.where(lane48 == 113, mean_col[:PACK], mean_col[PACK:2 * PACK])
    lbuf[...] = jnp.where((lane48 == 113) | (lane48 == 114), means, out)
    lbuf[:8, :] = jnp.where(lanes_of(8) == 115, mean_col[2 * PACK:], lbuf[:8, :])

    def copy3(src, o, dev, n):
        return pltpu.make_async_remote_copy(
            src_ref=src, dst_ref=r3buf.at[o], send_sem=send3.at[n], recv_sem=recv3.at[o],
            device_id=dev, device_id_type=pl.DeviceIdType.MESH)

    near, far = (6, 2, 7, 1), (4, 3, 5)

    def beyond(t):
        return device((x + 2) % 4, (y + t) % 8, z, core)

    sent3 = [copy3(lbuf, own, partner3(t)[1], t) for t in far]
    for t in near:
        sent3.append(copy3(lbuf, own, beyond(t), 8 + t))
        sent3.append(copy3(lbuf, own, partner3(t)[1], t))
    sent3.append(copy3(lbuf, own, across, 0))
    for copy in sent3:
        copy.start()
    r3buf[own] = lbuf[...]
    for t in far:
        o = partner3(t)[0]
        copy3(lbuf, o, across, 8 + t).wait_recv()
        copy = copy3(r3buf.at[o], o, across, 8 + t)
        copy.start()
        sent3.append(copy)
    for t in near:
        copy3(lbuf, partner3(t)[0], across, 8 + t).wait_recv()
    for t in range(8):
        copy3(lbuf, place((x_hi + 1) % 2, (y + t) % 8), across, 0).wait_recv()

    loop(1, GROUP, lambda t: copy1(t).wait_send())
    for copy in sent2:
        copy.wait_send()
    for copy in sent3:
        copy.wait_send()


def spread(packed_ref, factor_ref, mean_ref):
    keep = mean_ref.shape[1]
    for o in range(0, 16, 2):
        turned = []
        for i in range(2):
            mine3 = packed_ref[o + i]
            turn = pltpu.roll(mine3, LANES - HEAD - 1, 1)
            extra = pltpu.roll(mine3[:8, :], LANES - 116 + PACK, 1)
            lane = lanes_of(PACK)
            turn = jnp.where((lane >= rows_of(PACK)) & (lane < HEAD + 3), turn, 0.0)
            lane8 = lanes_of(8)
            extra = jnp.where((lane8 >= PACK + rows_of(8)) & (lane8 < HEAD), extra, 0.0)
            turned.append(jnp.concatenate([turn, extra, jnp.zeros((8, LANES), jnp.float32)], axis=0))
        both = (turned[0] + pltpu.roll(turned[1], 64, 1)).T
        for i in range(2):
            head = both[64 * i:64 * i + 64, :]
            factor_ref[0:HEAD, o + i, 0:64] = head[:HEAD, :]
            factor_ref[0:HEAD, o + i, 64:keep] = jnp.zeros((HEAD, keep - 64), jnp.float32)
            factor_ref[HEAD:keep, o + i, :] = unpack_tail(packed_ref[o + i])[:keep - HEAD, :keep]
            mean_ref[o + i:o + i + 1, 0:PACK] = head[HEAD:HEAD + 1, :PACK]
            mean_ref[o + i:o + i + 1, PACK:2 * PACK] = head[HEAD + 1:HEAD + 2, :PACK]
            mean_ref[o + i:o + i + 1, 2 * PACK:keep] = head[HEAD + 2:HEAD + 3, :keep - 2 * PACK]


def local(features, channel_index):
    batches, imgs, positions, width = features.shape
    keep = channel_index.shape[0]
    images = batches * imgs
    image_total = images * lax.axis_size("pos") * lax.axis_size("grp")
    owned = positions // lax.axis_size("pos")
    f32, bf16 = jnp.float32, jnp.bfloat16
    vmem = pl.BlockSpec(memory_space=pltpu.VMEM)
    packed = pl.pallas_call(
        lambda *refs: kernel(image_total, *refs),
        out_shape=pltpu.VMEM((owned, PACK, LANES), f32),
        in_specs=[pl.BlockSpec(memory_space=pl.ANY)] * 2,
        out_specs=vmem,
        scratch_shapes=[
            pltpu.VMEM((1, keep), jnp.int32),
            pltpu.VMEM((8, LANES), jnp.int32),
            pltpu.VMEM((images, width, positions), bf16),
            pltpu.VMEM((images * positions, LANES), f32),
            pltpu.VMEM((GROUP, SHARE * images, LANES), bf16),
            pltpu.VMEM((GROUP, SHARE * images, LANES), bf16),
            pltpu.VMEM((SHARE, PACK, LANES), f32),
            pltpu.VMEM((SHARE, PACK, LANES), f32),
            pltpu.VMEM((PACK, LANES), f32),
            pltpu.SemaphoreType.DMA,
            pltpu.SemaphoreType.DMA((images,)),
            pltpu.SemaphoreType.DMA((GROUP,)),
            pltpu.SemaphoreType.DMA((GROUP,)),
            pltpu.SemaphoreType.DMA((16,)),
            pltpu.SemaphoreType.DMA((16,)),
            pltpu.SemaphoreType.DMA((16,)),
            pltpu.SemaphoreType.DMA((16,)),
        ],
        compiler_params=pltpu.CompilerParams(
            collective_id=0, has_side_effects=True, vmem_limit_bytes=60 * 1024 * 1024),
        name="gaussian_stats",
    )(channel_index.reshape(1, keep), pltpu.with_memory_space_constraint(jnp.swapaxes(features, 2, 3), pltpu.HBM))
    factor, mean_vec = pl.pallas_call(
        spread,
        out_shape=(jax.ShapeDtypeStruct((keep, owned, keep), f32), jax.ShapeDtypeStruct((owned, keep), f32)),
        in_specs=[vmem],
        out_specs=(vmem, vmem),
        compiler_params=pltpu.CompilerParams(vmem_limit_bytes=16 * 1024 * 1024),
        name="spread",
    )(packed)
    return jnp.swapaxes(factor, 0, 1), mean_vec


def solution(mesh):
    return jax.shard_map(
        local,
        mesh=mesh,
        in_specs=(P(None, ("grp", "pos"), None, None), P()),
        out_specs=(P("pos", None, None), P("pos", None)),
        check_vma=False,
    )
```

```python
import jax
import jax.numpy as jnp
from jax import lax
from jax.experimental import pallas as pl
from jax.experimental.pallas import tpu as pltpu
from jax.sharding import PartitionSpec as P

RIDGE = 0.01
LANES = 128
NX, NY, NZ = 4, 8, 8
GROUP = 32
SHARE = 16
ROWS = 104
HEAD, PACK = 56, 48


def lanes_of(rows):
    return lax.broadcasted_iota(jnp.int32, (rows, LANES), 1)


def rows_of(rows):
    return lax.broadcasted_iota(jnp.int32, (rows, LANES), 0)


def pack(low, up):
    row, lane = rows_of(PACK), lanes_of(PACK)
    corner = pltpu.roll(up[PACK:HEAD, :], 116 - PACK, 1)
    lane8 = lanes_of(8)
    out = jnp.where(lane <= HEAD + row, low[HEAD:ROWS, :], pltpu.roll(up[:PACK, :], HEAD + 1, 1))
    first = jnp.where((lane8 >= 116) & (lane8 < 124), corner, out[:8, :])
    return jnp.concatenate([first, out[8:, :]], axis=0)


def unpack_head(packed):
    head = jnp.concatenate(
        [pltpu.roll(packed, LANES - HEAD - 1, 1), pltpu.roll(packed[:8, :], LANES - 116 + PACK, 1)], axis=0)
    lane = lanes_of(HEAD)
    return jnp.where((lane >= rows_of(HEAD)) & (lane < HEAD), head, 0.0)


def unpack_tail(packed):
    return jnp.where(lanes_of(PACK) <= HEAD + rows_of(PACK), packed, 0.0)


def ring(d, n):
    return min(d, n - d)


ORDER1 = [t for t in (8 * dx + 4 * dz + 2 * dy + dc for dz, dy in ((1, 1), (1, 0), (0, 1), (0, 0)) for dc in range(2)
                      for dx in (2, 1, 3, 0)) if t]
ORDER3 = sorted(range(1, 8), key=lambda t: -ring(t, 8))
ORDER2 = sorted(range(1, 16), key=lambda t: -2 * (ring(t // 4, 4) + ring(t % 4, 4)))


def kernel(image_total, idx_ref, feat_ref, factor_ref, mean_ref,
           idx, idx_pad, feat, wide, sbuf, rbuf, pbuf, r2buf, lbuf, r3buf,
           idx_sem, load_sem, send1, recv1, send2, recv2, send3, recv3):
    batches, imgs, width, positions = feat_ref.shape
    images = batches * imgs
    keep = idx_ref.shape[1]
    grp = lax.axis_index("grp")
    pos = lax.axis_index("pos")
    y, x_hi = grp // 2, grp % 2
    x_lo, z, core = pos // (2 * NZ), (pos // 2) % NZ, pos % 2
    x = 2 * x_hi + x_lo
    y_hi, y_lo = y // 2, y % 2
    z_hi, z_lo = z // 2, z % 2

    def device(xx, yy, zz, cc):
        return {"grp": yy * 2 + xx // 2, "pos": ((xx % 2) * NZ + zz) * 2 + cc}

    def partner1(t):
        xx = (x + t // 8) % 4
        zl = (z_lo + (t // 4) % 2) % 2
        yl = (y_lo + (t // 2) % 2) % 2
        cc = (core + t % 2) % 2
        return ((xx * 2 + zl) * 2 + yl) * 2 + cc, device(xx, 2 * y_hi + yl, 2 * z_hi + zl, cc)

    def partner2(t):
        q = ((z_hi + t // 4) % 4) * 4 + (y_hi + t % 4) % 4
        return q, device(x, 2 * (q % 4) + y_lo, 2 * (q // 4) + z_lo, core)

    def place(xh, yy):
        return xh * 8 + (yy % 2) * 4 + yy // 2

    def partner3(t):
        yy = (y + t) % 8
        return place(x_hi, yy), device(x, yy, z, core)

    across = device((x + 2) % 4, y, z, core)

    me = ((x * 2 + z_lo) * 2 + y_lo) * 2 + core
    mine = z_hi * 4 + y_hi
    own = x_hi * 8 + y_lo * 4 + y_hi

    idx_copy = pltpu.make_async_copy(idx_ref, idx, idx_sem)
    idx_copy.start()
    copies = []
    for b in range(batches):
        for i in range(imgs):
            k = b * imgs + i
            c = pltpu.make_async_copy(feat_ref.at[b, i], feat.at[k], load_sem.at[k])
            c.start()
            copies.append(c)

    barrier = pltpu.get_barrier_semaphore()

    greetings = [partner2(t)[1] for t in ORDER2] + [partner1(t)[1] for t in ORDER1]

    def greet(devices):
        for dev in devices:
            pl.semaphore_signal(barrier, inc=1, device_id=dev, device_id_type=pl.DeviceIdType.MESH)

    greet(greetings)

    idx_pad[...] = jnp.full(idx_pad.shape, -1, jnp.int32)
    idx_copy.wait()
    idx_pad[0:1, 0:keep] = idx[...]
    selector = jnp.where(
        lax.broadcasted_iota(jnp.int32, (4 * LANES, LANES), 0) == idx_pad[0:1, :], 1.0, 0.0
    ).T[:, :width].astype(jnp.bfloat16)
    for k in range(images):
        copies[k].wait()
        picked = jnp.dot(selector, feat[k], preferred_element_type=jnp.float32)
        wide[pl.ds(k, positions, stride=images), :] = picked.T
    chunk = 4 * images
    ones_lane = lax.broadcasted_iota(jnp.int32, (chunk, LANES), 1) == keep
    for d in range(GROUP):
        xx, zl, yl, cc = d // 8, (d // 4) % 2, (d // 2) % 2, d % 2
        for zh in range(4):
            first = 16 * (((xx % 2) * NZ + 2 * zh + zl) * 2 + cc) + 8 * (xx // 2) + 4 * yl
            piece = wide[first * images:first * images + chunk, :]
            sbuf[d, zh * chunk:(zh + 1) * chunk, :] = jnp.where(ones_lane, 1.0, piece).astype(jnp.bfloat16)

    pl.semaphore_wait(barrier, GROUP - 1 + 15)

    def copy1(t):
        d, dev = partner1(t)
        return pltpu.make_async_remote_copy(
            src_ref=sbuf.at[d], dst_ref=rbuf.at[me], send_sem=send1.at[t], recv_sem=recv1.at[me],
            device_id=dev, device_id_type=pl.DeviceIdType.MESH)

    def got1(t):
        s, dev = partner1(t)
        return pltpu.make_async_remote_copy(
            src_ref=sbuf.at[s], dst_ref=rbuf.at[s], send_sem=send1.at[t], recv_sem=recv1.at[s],
            device_id=dev, device_id_type=pl.DeviceIdType.MESH)

    def loop(lo, hi, act):
        def body(t, carry):
            act(t)
            return carry
        lax.fori_loop(lo, hi, body, 0)

    for t in ORDER1:
        copy1(t).start()
    rbuf[me] = sbuf[me]
    loop(1, GROUP, lambda t: got1(t).wait_recv())

    half = (lax.broadcasted_iota(jnp.int32, (16, LANES), 0) < images).astype(jnp.float32)
    even = half.astype(jnp.bfloat16)
    odd = (1.0 - half).astype(jnp.bfloat16)

    def copy2(q, n):
        dev = device(x, 2 * (q % 4) + y_lo, 2 * (q // 4) + z_lo, core)
        return pltpu.make_async_remote_copy(
            src_ref=pbuf.at[q], dst_ref=r2buf.at[mine], send_sem=send2.at[n], recv_sem=recv2.at[mine],
            device_id=dev, device_id_type=pl.DeviceIdType.MESH)

    sent2 = []
    for dz, dy in ((2, 1), (2, 0), (1, 1), (3, 1), (1, 0), (3, 0), (0, 1), (0, 0)):
        j = ((z_hi + dz) % 4) * 2 + (y_hi // 2 + dy) % 2
        tile = rbuf[:, pl.ds(pl.multiple_of(16 * j, 16), 16), :]
        flat = tile.reshape(GROUP * 16, LANES)
        rhs = jnp.concatenate(
            [(tile * even[None]).reshape(GROUP * 16, LANES), (tile * odd[None]).reshape(GROUP * 16, LANES)], axis=1)
        both = lax.dot_general(flat, rhs, (((0,), (0,)), ((), ())), preferred_element_type=jnp.float32)
        pbuf[2 * j] = pack(both[:, :LANES], both[:, :LANES])
        pbuf[2 * j + 1] = pack(both[:, LANES:], both[:, LANES:])
        for q in ([2 * j, 2 * j + 1] if dz or dy else [2 * j + 1 - y_hi % 2]):
            copy = copy2(q, len(sent2))
            copy.start()
            sent2.append(copy)

    def got2(t):
        s, dev = partner2(t)
        return pltpu.make_async_remote_copy(
            src_ref=pbuf.at[s], dst_ref=r2buf.at[s], send_sem=send2.at[t], recv_sem=recv2.at[s],
            device_id=dev, device_id_type=pl.DeviceIdType.MESH)

    r2buf[mine] = pbuf[mine]
    loop(1, 16, lambda t: got2(t).wait_recv())
    packed = jnp.sum(r2buf[...], axis=0)
    half_total = jnp.concatenate(
        [unpack_head(packed), unpack_tail(packed), jnp.zeros((LANES - ROWS, LANES), jnp.float32)], axis=0)
    row128, lane128 = rows_of(LANES), lanes_of(LANES)
    total = (half_total + jnp.where(row128 == lane128, 0.0, half_total.T))[:ROWS, :]

    row = lax.broadcasted_iota(jnp.int32, (ROWS, LANES), 0)
    lane = lax.broadcasted_iota(jnp.int32, (ROWS, LANES), 1)
    mean_row = total[keep:keep + 1, :] / image_total
    mean_col = total[:, keep:keep + 1] / image_total
    cov = (total - (image_total * mean_col) * mean_row) / (image_total - 1)
    cov = cov + jnp.where(row == lane, RIDGE, 0.0)
    cov = jnp.where((row < keep) & (lane < keep), cov, jnp.where(row == lane, 1.0, 0.0))
    blocks = [cov[8 * i:8 * i + 8, :] for i in range(ROWS // 8)]
    sub = lax.broadcasted_iota(jnp.int32, (8, LANES), 0)

    def spread_row(v, k):
        return jnp.broadcast_to(v[k:k + 1, :], (8, LANES))

    upper = []
    count = ROWS // 8
    for j in range(count):
        cols = [[jnp.broadcast_to(blocks[i][:, 8 * j + k:8 * j + k + 1], (8, LANES)) for k in range(8)]
                for i in range(j, count)]
        root = jnp.zeros((8, LANES), jnp.float32)
        for k in range(8):
            pivot = spread_row(cols[0][k], k)
            inv = 1.0 / pivot
            root = jnp.where(sub == k, lax.rsqrt(pivot), root)
            main_row = spread_row(blocks[j], k) * inv
            col_rows = [spread_row(cols[0][m], k) * inv for m in range(k + 1, 8)]
            for i in range(j, count):
                left = cols[i - j][k]
                if i == j:
                    left = jnp.where(sub > k, left, 0.0)
                blocks[i] = blocks[i] - left * main_row
                for m in range(k + 1, 8):
                    cols[i - j][m] = cols[i - j][m] - left * col_rows[m - k - 1]
        upper.append(blocks[j] * root)
    full = jnp.concatenate(upper + [jnp.zeros((LANES - ROWS, LANES), jnp.float32)], axis=0)
    full = jnp.where(lane128 >= row128, full, 0.0)
    lower = full.T
    out = pack(lower, full)
    lane48 = lanes_of(PACK)
    means = jnp.where(lane48 == 113, mean_col[:PACK], mean_col[PACK:2 * PACK])
    lbuf[...] = jnp.where((lane48 == 113) | (lane48 == 114), means, out)
    lbuf[:8, :] = jnp.where(lanes_of(8) == 115, mean_col[2 * PACK:], lbuf[:8, :])

    def copy3(src, o, dev, n):
        return pltpu.make_async_remote_copy(
            src_ref=src, dst_ref=r3buf.at[o], send_sem=send3.at[n], recv_sem=recv3.at[o],
            device_id=dev, device_id_type=pl.DeviceIdType.MESH)

    near, far = (6, 2, 7, 1), (4, 3, 5)

    def beyond(t):
        return device((x + 2) % 4, (y + t) % 8, z, core)

    sent3 = [copy3(lbuf, own, partner3(t)[1], t) for t in far]
    for t in near:
        sent3.append(copy3(lbuf, own, beyond(t), 8 + t))
        sent3.append(copy3(lbuf, own, partner3(t)[1], t))
    sent3.append(copy3(lbuf, own, across, 0))
    for copy in sent3:
        copy.start()
    r3buf[own] = lbuf[...]
    for t in far:
        o = partner3(t)[0]
        copy3(lbuf, o, across, 8 + t).wait_recv()
        copy = copy3(r3buf.at[o], o, across, 8 + t)
        copy.start()
        sent3.append(copy)
    for o in range(0, 16, 2):
        for i in (o, o + 1):
            ahead = (2 * (i % 4) + (i // 4) % 2 + 8 - y) % 8
            here = jnp.where(i // 8 == x_hi, 1, 0)
            known = jnp.where((ahead == 0) | ((ahead >= 3) & (ahead <= 5)), 1, 0) * here

            @pl.when(known == 0)
            def _():
                copy3(lbuf, i, across, 0).wait_recv()

        turned = []
        for i in range(2):
            mine3 = r3buf[o + i]
            turn = pltpu.roll(mine3, LANES - HEAD - 1, 1)
            extra = pltpu.roll(mine3[:8, :], LANES - 116 + PACK, 1)
            lane = lanes_of(PACK)
            turn = jnp.where((lane >= rows_of(PACK)) & (lane < HEAD + 3), turn, 0.0)
            lane8 = lanes_of(8)
            extra = jnp.where((lane8 >= PACK + rows_of(8)) & (lane8 < HEAD), extra, 0.0)
            turned.append(jnp.concatenate([turn, extra, jnp.zeros((8, LANES), jnp.float32)], axis=0))
        both = (turned[0] + pltpu.roll(turned[1], 64, 1)).T
        for i in range(2):
            head = both[64 * i:64 * i + 64, :]
            factor_ref[0:HEAD, o + i, 0:64] = head[:HEAD, :]
            factor_ref[0:HEAD, o + i, 64:keep] = jnp.zeros((HEAD, keep - 64), jnp.float32)
            factor_ref[HEAD:keep, o + i, :] = unpack_tail(r3buf[o + i])[:keep - HEAD, :keep]
            mean_ref[o + i:o + i + 1, 0:PACK] = head[HEAD:HEAD + 1, :PACK]
            mean_ref[o + i:o + i + 1, PACK:2 * PACK] = head[HEAD + 1:HEAD + 2, :PACK]
            mean_ref[o + i:o + i + 1, 2 * PACK:keep] = head[HEAD + 2:HEAD + 3, :keep - 2 * PACK]

    loop(1, GROUP, lambda t: copy1(t).wait_send())
    for copy in sent2:
        copy.wait_send()
    for copy in sent3:
        copy.wait_send()


def store(factor_in, mean_in, factor_ref, mean_ref, sems):
    copies = [pltpu.make_async_copy(factor_in, factor_ref, sems.at[0]),
              pltpu.make_async_copy(mean_in, mean_ref, sems.at[1])]
    for copy in copies:
        copy.start()
    for copy in copies:
        copy.wait()


def local(features, channel_index):
    batches, imgs, positions, width = features.shape
    keep = channel_index.shape[0]
    images = batches * imgs
    image_total = images * lax.axis_size("pos") * lax.axis_size("grp")
    owned = positions // lax.axis_size("pos")
    f32, bf16 = jnp.float32, jnp.bfloat16
    vmem = pl.BlockSpec(memory_space=pltpu.VMEM)
    factor, mean_vec = pl.pallas_call(
        lambda *refs: kernel(image_total, *refs),
        out_shape=(pltpu.VMEM((keep, owned, keep), f32), pltpu.VMEM((owned, keep), f32)),
        in_specs=[pl.BlockSpec(memory_space=pl.ANY)] * 2,
        out_specs=(vmem, vmem),
        scratch_shapes=[
            pltpu.VMEM((1, keep), jnp.int32),
            pltpu.VMEM((8, LANES), jnp.int32),
            pltpu.VMEM((images, width, positions), bf16),
            pltpu.VMEM((images * positions, LANES), f32),
            pltpu.VMEM((GROUP, SHARE * images, LANES), bf16),
            pltpu.VMEM((GROUP, SHARE * images, LANES), bf16),
            pltpu.VMEM((SHARE, PACK, LANES), f32),
            pltpu.VMEM((SHARE, PACK, LANES), f32),
            pltpu.VMEM((PACK, LANES), f32),
            pltpu.VMEM((SHARE, PACK, LANES), f32),
            pltpu.SemaphoreType.DMA,
            pltpu.SemaphoreType.DMA((images,)),
            pltpu.SemaphoreType.DMA((GROUP,)),
            pltpu.SemaphoreType.DMA((GROUP,)),
            pltpu.SemaphoreType.DMA((16,)),
            pltpu.SemaphoreType.DMA((16,)),
            pltpu.SemaphoreType.DMA((16,)),
            pltpu.SemaphoreType.DMA((16,)),
        ],
        compiler_params=pltpu.CompilerParams(
            collective_id=0, has_side_effects=True, vmem_limit_bytes=60 * 1024 * 1024),
        name="gaussian_stats",
    )(channel_index.reshape(1, keep), pltpu.with_memory_space_constraint(jnp.swapaxes(features, 2, 3), pltpu.HBM))
    factor, mean_vec = pl.pallas_call(
        store,
        out_shape=(jax.ShapeDtypeStruct((keep, owned, keep), f32), jax.ShapeDtypeStruct((owned, keep), f32)),
        in_specs=[vmem, vmem],
        out_specs=(pl.BlockSpec(memory_space=pl.ANY), pl.BlockSpec(memory_space=pl.ANY)),
        scratch_shapes=[pltpu.SemaphoreType.DMA((2,))],
        compiler_params=pltpu.CompilerParams(vmem_limit_bytes=16 * 1024 * 1024),
        name="store",
    )(factor, mean_vec)
    return jnp.swapaxes(factor, 0, 1), mean_vec


def solution(mesh):
    return jax.shard_map(
        local,
        mesh=mesh,
        in_specs=(P(None, ("grp", "pos"), None, None), P()),
        out_specs=(P("pos", None, None), P("pos", None)),
        check_vma=False,
    )
```

```python
import jax
import jax.numpy as jnp
from jax import lax
from jax.experimental import pallas as pl
from jax.experimental.pallas import tpu as pltpu
from jax.sharding import PartitionSpec as P

RIDGE = 0.01
LANES = 128
NX, NY, NZ = 4, 8, 8
GROUP = 32
SHARE = 16
ROWS = 104
HEAD, PACK = 56, 48


def lanes_of(rows):
    return lax.broadcasted_iota(jnp.int32, (rows, LANES), 1)


def rows_of(rows):
    return lax.broadcasted_iota(jnp.int32, (rows, LANES), 0)


def pack(low, up):
    row, lane = rows_of(PACK), lanes_of(PACK)
    corner = pltpu.roll(up[PACK:HEAD, :], 116 - PACK, 1)
    lane8 = lanes_of(8)
    out = jnp.where(lane <= HEAD + row, low[HEAD:ROWS, :], pltpu.roll(up[:PACK, :], HEAD + 1, 1))
    first = jnp.where((lane8 >= 116) & (lane8 < 124), corner, out[:8, :])
    return jnp.concatenate([first, out[8:, :]], axis=0)


def unpack_head(packed):
    head = jnp.concatenate(
        [pltpu.roll(packed, LANES - HEAD - 1, 1), pltpu.roll(packed[:8, :], LANES - 116 + PACK, 1)], axis=0)
    lane = lanes_of(HEAD)
    return jnp.where((lane >= rows_of(HEAD)) & (lane < HEAD), head, 0.0)


def unpack_tail(packed):
    return jnp.where(lanes_of(PACK) <= HEAD + rows_of(PACK), packed, 0.0)


def ring(d, n):
    return min(d, n - d)


ORDER1 = [t for t in (8 * dx + 4 * dz + 2 * dy + dc for dz, dy in ((1, 1), (1, 0), (0, 1), (0, 0)) for dc in range(2)
                      for dx in (2, 1, 3, 0)) if t]
ORDER3 = sorted(range(1, 8), key=lambda t: -ring(t, 8))
ORDER2 = sorted(range(1, 16), key=lambda t: -2 * (ring(t // 4, 4) + ring(t % 4, 4)))


def kernel(image_total, idx_ref, feat_ref, factor_ref, mean_ref,
           idx, idx_pad, feat, wide, sbuf, rbuf, pbuf, r2buf, lbuf, r3buf,
           idx_sem, load_sem, send1, recv1, send2, recv2, send3, recv3):
    batches, imgs, width, positions = feat_ref.shape
    images = batches * imgs
    keep = idx_ref.shape[1]
    grp = lax.axis_index("grp")
    pos = lax.axis_index("pos")
    y, x_hi = grp // 2, grp % 2
    x_lo, z, core = pos // (2 * NZ), (pos // 2) % NZ, pos % 2
    x = 2 * x_hi + x_lo
    y_hi, y_lo = y // 2, y % 2
    z_hi, z_lo = z // 2, z % 2

    def device(xx, yy, zz, cc):
        return {"grp": yy * 2 + xx // 2, "pos": ((xx % 2) * NZ + zz) * 2 + cc}

    def partner1(t):
        xx = (x + t // 8) % 4
        zl = (z_lo + (t // 4) % 2) % 2
        yl = (y_lo + (t // 2) % 2) % 2
        cc = (core + t % 2) % 2
        return ((xx * 2 + zl) * 2 + yl) * 2 + cc, device(xx, 2 * y_hi + yl, 2 * z_hi + zl, cc)

    def partner2(t):
        q = ((z_hi + t // 4) % 4) * 4 + (y_hi + t % 4) % 4
        return q, device(x, 2 * (q % 4) + y_lo, 2 * (q // 4) + z_lo, core)

    def place(xh, yy):
        return xh * 8 + (yy % 2) * 4 + yy // 2

    def partner3(t):
        yy = (y + t) % 8
        return place(x_hi, yy), device(x, yy, z, core)

    across = device((x + 2) % 4, y, z, core)

    me = ((x * 2 + z_lo) * 2 + y_lo) * 2 + core
    mine = z_hi * 4 + y_hi
    own = x_hi * 8 + y_lo * 4 + y_hi

    idx_copy = pltpu.make_async_copy(idx_ref, idx, idx_sem)
    idx_copy.start()
    copies = []
    for b in range(batches):
        for i in range(imgs):
            k = b * imgs + i
            c = pltpu.make_async_copy(feat_ref.at[b, i], feat.at[k], load_sem.at[k])
            c.start()
            copies.append(c)

    barrier = pltpu.get_barrier_semaphore()

    greetings = [partner2(t)[1] for t in ORDER2] + [partner1(t)[1] for t in ORDER1]

    def greet(devices):
        for dev in devices:
            pl.semaphore_signal(barrier, inc=1, device_id=dev, device_id_type=pl.DeviceIdType.MESH)

    greet(greetings)

    idx_pad[...] = jnp.full(idx_pad.shape, -1, jnp.int32)
    idx_copy.wait()
    idx_pad[0:1, 0:keep] = idx[...]
    selector = jnp.where(
        lax.broadcasted_iota(jnp.int32, (4 * LANES, LANES), 0) == idx_pad[0:1, :], 1.0, 0.0
    ).T[:, :width].astype(jnp.bfloat16)
    for k in range(images):
        copies[k].wait()
        picked = jnp.dot(selector, feat[k], preferred_element_type=jnp.float32)
        wide[pl.ds(k, positions, stride=images), :] = picked.T
    chunk = 4 * images
    ones_lane = lax.broadcasted_iota(jnp.int32, (chunk, LANES), 1) == keep
    for d in range(GROUP):
        xx, zl, yl, cc = d // 8, (d // 4) % 2, (d // 2) % 2, d % 2
        for zh in range(4):
            first = 16 * (((xx % 2) * NZ + 2 * zh + zl) * 2 + cc) + 8 * (xx // 2) + 4 * yl
            piece = wide[first * images:first * images + chunk, :]
            sbuf[d, zh * chunk:(zh + 1) * chunk, :] = jnp.where(ones_lane, 1.0, piece).astype(jnp.bfloat16)

    pl.semaphore_wait(barrier, GROUP - 1 + 15)

    def copy1(t):
        d, dev = partner1(t)
        return pltpu.make_async_remote_copy(
            src_ref=sbuf.at[d], dst_ref=rbuf.at[me], send_sem=send1.at[t], recv_sem=recv1.at[me],
            device_id=dev, device_id_type=pl.DeviceIdType.MESH)

    def got1(t):
        s, dev = partner1(t)
        return pltpu.make_async_remote_copy(
            src_ref=sbuf.at[s], dst_ref=rbuf.at[s], send_sem=send1.at[t], recv_sem=recv1.at[s],
            device_id=dev, device_id_type=pl.DeviceIdType.MESH)

    def loop(lo, hi, act):
        def body(t, carry):
            act(t)
            return carry
        lax.fori_loop(lo, hi, body, 0)

    for t in ORDER1:
        copy1(t).start()
    rbuf[me] = sbuf[me]
    loop(1, GROUP, lambda t: got1(t).wait_recv())

    half = (lax.broadcasted_iota(jnp.int32, (16, LANES), 0) < images).astype(jnp.float32)
    even = half.astype(jnp.bfloat16)
    odd = (1.0 - half).astype(jnp.bfloat16)

    def copy2(q, n):
        dev = device(x, 2 * (q % 4) + y_lo, 2 * (q // 4) + z_lo, core)
        return pltpu.make_async_remote_copy(
            src_ref=pbuf.at[q], dst_ref=r2buf.at[mine], send_sem=send2.at[n], recv_sem=recv2.at[mine],
            device_id=dev, device_id_type=pl.DeviceIdType.MESH)

    sent2 = []
    for dz, dy in ((2, 1), (2, 0), (1, 1), (3, 1), (1, 0), (3, 0), (0, 1), (0, 0)):
        j = ((z_hi + dz) % 4) * 2 + (y_hi // 2 + dy) % 2
        tile = rbuf[:, pl.ds(pl.multiple_of(16 * j, 16), 16), :]
        flat = tile.reshape(GROUP * 16, LANES)
        rhs = jnp.concatenate(
            [(tile * even[None]).reshape(GROUP * 16, LANES), (tile * odd[None]).reshape(GROUP * 16, LANES)], axis=1)
        both = lax.dot_general(flat, rhs, (((0,), (0,)), ((), ())), preferred_element_type=jnp.float32)
        pbuf[2 * j] = pack(both[:, :LANES], both[:, :LANES])
        pbuf[2 * j + 1] = pack(both[:, LANES:], both[:, LANES:])
        for q in ([2 * j, 2 * j + 1] if dz or dy else [2 * j + 1 - y_hi % 2]):
            copy = copy2(q, len(sent2))
            copy.start()
            sent2.append(copy)

    def got2(t):
        s, dev = partner2(t)
        return pltpu.make_async_remote_copy(
            src_ref=pbuf.at[s], dst_ref=r2buf.at[s], send_sem=send2.at[t], recv_sem=recv2.at[s],
            device_id=dev, device_id_type=pl.DeviceIdType.MESH)

    r2buf[mine] = pbuf[mine]
    loop(1, 16, lambda t: got2(t).wait_recv())
    packed = jnp.sum(r2buf[...], axis=0)
    half_total = jnp.concatenate(
        [unpack_head(packed), unpack_tail(packed), jnp.zeros((LANES - ROWS, LANES), jnp.float32)], axis=0)
    row128, lane128 = rows_of(LANES), lanes_of(LANES)
    total = (half_total + jnp.where(row128 == lane128, 0.0, half_total.T))[:ROWS, :]

    row = lax.broadcasted_iota(jnp.int32, (ROWS, LANES), 0)
    lane = lax.broadcasted_iota(jnp.int32, (ROWS, LANES), 1)
    mean_row = total[keep:keep + 1, :] / image_total
    mean_col = total[:, keep:keep + 1] / image_total
    cov = (total - (image_total * mean_col) * mean_row) / (image_total - 1)
    cov = cov + jnp.where(row == lane, RIDGE, 0.0)
    cov = jnp.where((row < keep) & (lane < keep), cov, jnp.where(row == lane, 1.0, 0.0))
    blocks = [cov[8 * i:8 * i + 8, :] for i in range(ROWS // 8)]
    sub = lax.broadcasted_iota(jnp.int32, (8, LANES), 0)

    def spread_row(v, k):
        return jnp.broadcast_to(v[k:k + 1, :], (8, LANES))

    upper = []
    count = ROWS // 8
    for j in range(count):
        cols = [[jnp.broadcast_to(blocks[i][:, 8 * j + k:8 * j + k + 1], (8, LANES)) for k in range(8)]
                for i in range(j, count)]
        root = jnp.zeros((8, LANES), jnp.float32)
        for k in range(8):
            pivot = spread_row(cols[0][k], k)
            inv = 1.0 / pivot
            root = jnp.where(sub == k, lax.rsqrt(pivot), root)
            main_row = spread_row(blocks[j], k) * inv
            col_rows = [spread_row(cols[0][m], k) * inv for m in range(k + 1, 8)]
            for i in range(j, count):
                left = cols[i - j][k]
                if i == j:
                    left = jnp.where(sub > k, left, 0.0)
                blocks[i] = blocks[i] - left * main_row
                for m in range(k + 1, 8):
                    cols[i - j][m] = cols[i - j][m] - left * col_rows[m - k - 1]
        upper.append(blocks[j] * root)
    full = jnp.concatenate(upper + [jnp.zeros((LANES - ROWS, LANES), jnp.float32)], axis=0)
    full = jnp.where(lane128 >= row128, full, 0.0)
    lower = full.T
    out = pack(lower, full)
    lane48 = lanes_of(PACK)
    means = jnp.where(lane48 == 113, mean_col[:PACK], mean_col[PACK:2 * PACK])
    lbuf[...] = jnp.where((lane48 == 113) | (lane48 == 114), means, out)
    lbuf[:8, :] = jnp.where(lanes_of(8) == 115, mean_col[2 * PACK:], lbuf[:8, :])

    def copy3(src, o, dev, n):
        return pltpu.make_async_remote_copy(
            src_ref=src, dst_ref=r3buf.at[o], send_sem=send3.at[n], recv_sem=recv3.at[o],
            device_id=dev, device_id_type=pl.DeviceIdType.MESH)

    near, far = (6, 2, 7, 1), (4, 3, 5)

    def beyond(t):
        return device((x + 2) % 4, (y + t) % 8, z, core)

    sent3 = [copy3(lbuf, own, partner3(t)[1], t) for t in far]
    for t in near:
        sent3.append(copy3(lbuf, own, beyond(t), 8 + t))
        sent3.append(copy3(lbuf, own, partner3(t)[1], t))
    sent3.append(copy3(lbuf, own, across, 0))
    for copy in sent3:
        copy.start()
    r3buf[own] = lbuf[...]
    for t in far:
        o = partner3(t)[0]
        copy3(lbuf, o, across, 8 + t).wait_recv()
        copy = copy3(r3buf.at[o], o, across, 8 + t)
        copy.start()
        sent3.append(copy)
    for o in range(0, 16, 2):
        for i in (o, o + 1):
            ahead = (2 * (i % 4) + (i // 4) % 2 + 8 - y) % 8
            here = jnp.where(i // 8 == x_hi, 1, 0)
            known = jnp.where((ahead == 0) | ((ahead >= 3) & (ahead <= 5)), 1, 0) * here

            @pl.when(known == 0)
            def _():
                copy3(lbuf, i, across, 0).wait_recv()

        turned = []
        for i in range(2):
            mine3 = r3buf[o + i]
            turn = pltpu.roll(mine3, LANES - HEAD - 1, 1)
            extra = pltpu.roll(mine3[:8, :], LANES - 116 + PACK, 1)
            lane = lanes_of(PACK)
            turn = jnp.where((lane >= rows_of(PACK)) & (lane < HEAD + 3), turn, 0.0)
            lane8 = lanes_of(8)
            extra = jnp.where((lane8 >= PACK + rows_of(8)) & (lane8 < HEAD), extra, 0.0)
            turned.append(jnp.concatenate([turn, extra, jnp.zeros((8, LANES), jnp.float32)], axis=0))
        both = (turned[0] + pltpu.roll(turned[1], 64, 1)).T
        for i in range(2):
            head = both[64 * i:64 * i + 64, :]
            factor_ref[0:HEAD, o + i, 0:64] = head[:HEAD, :]
            factor_ref[0:HEAD, o + i, 64:keep] = jnp.zeros((HEAD, keep - 64), jnp.float32)
            factor_ref[HEAD:ROWS, o + i, :] = unpack_tail(r3buf[o + i])[:, :keep]
            mean_ref[o + i:o + i + 1, 0:PACK] = head[HEAD:HEAD + 1, :PACK]
            mean_ref[o + i:o + i + 1, PACK:2 * PACK] = head[HEAD + 1:HEAD + 2, :PACK]
            mean_ref[o + i:o + i + 1, 2 * PACK:keep] = head[HEAD + 2:HEAD + 3, :keep - 2 * PACK]

    loop(1, GROUP, lambda t: copy1(t).wait_send())
    for copy in sent2:
        copy.wait_send()
    for copy in sent3:
        copy.wait_send()


def store(factor_in, mean_in, factor_ref, mean_ref, sems):
    copies = [pltpu.make_async_copy(factor_in.at[pl.ds(0, factor_ref.shape[0])], factor_ref, sems.at[0]),
              pltpu.make_async_copy(mean_in, mean_ref, sems.at[1])]
    for copy in copies:
        copy.start()
    for copy in copies:
        copy.wait()


def local(features, channel_index):
    batches, imgs, positions, width = features.shape
    keep = channel_index.shape[0]
    images = batches * imgs
    image_total = images * lax.axis_size("pos") * lax.axis_size("grp")
    owned = positions // lax.axis_size("pos")
    f32, bf16 = jnp.float32, jnp.bfloat16
    vmem = pl.BlockSpec(memory_space=pltpu.VMEM)
    factor, mean_vec = pl.pallas_call(
        lambda *refs: kernel(image_total, *refs),
        out_shape=(pltpu.VMEM((ROWS, owned, keep), f32), pltpu.VMEM((owned, keep), f32)),
        in_specs=[pl.BlockSpec(memory_space=pl.ANY)] * 2,
        out_specs=(vmem, vmem),
        scratch_shapes=[
            pltpu.VMEM((1, keep), jnp.int32),
            pltpu.VMEM((8, LANES), jnp.int32),
            pltpu.VMEM((images, width, positions), bf16),
            pltpu.VMEM((images * positions + 8, LANES), f32),
            pltpu.VMEM((GROUP, SHARE * images, LANES), bf16),
            pltpu.VMEM((GROUP, SHARE * images, LANES), bf16),
            pltpu.VMEM((SHARE, PACK, LANES), f32),
            pltpu.VMEM((SHARE, PACK, LANES), f32),
            pltpu.VMEM((PACK, LANES), f32),
            pltpu.VMEM((SHARE, PACK, LANES), f32),
            pltpu.SemaphoreType.DMA,
            pltpu.SemaphoreType.DMA((images,)),
            pltpu.SemaphoreType.DMA((GROUP,)),
            pltpu.SemaphoreType.DMA((GROUP,)),
            pltpu.SemaphoreType.DMA((16,)),
            pltpu.SemaphoreType.DMA((16,)),
            pltpu.SemaphoreType.DMA((16,)),
            pltpu.SemaphoreType.DMA((16,)),
        ],
        compiler_params=pltpu.CompilerParams(
            collective_id=0, has_side_effects=True, vmem_limit_bytes=60 * 1024 * 1024),
        name="gaussian_stats",
    )(channel_index.reshape(1, keep), pltpu.with_memory_space_constraint(jnp.swapaxes(features, 2, 3), pltpu.HBM))
    factor, mean_vec = pl.pallas_call(
        store,
        out_shape=(jax.ShapeDtypeStruct((keep, owned, keep), f32), jax.ShapeDtypeStruct((owned, keep), f32)),
        in_specs=[vmem, vmem],
        out_specs=(pl.BlockSpec(memory_space=pl.ANY), pl.BlockSpec(memory_space=pl.ANY)),
        scratch_shapes=[pltpu.SemaphoreType.DMA((2,))],
        compiler_params=pltpu.CompilerParams(vmem_limit_bytes=16 * 1024 * 1024),
        name="store",
    )(factor, mean_vec)
    return jnp.swapaxes(factor, 0, 1), mean_vec


def solution(mesh):
    return jax.shard_map(
        local,
        mesh=mesh,
        in_specs=(P(None, ("grp", "pos"), None, None), P()),
        out_specs=(P("pos", None, None), P("pos", None)),
        check_vma=False,
    )
```
